32 devices in a mesh: dp: 4 (over z), ctx: 4 (over y, x), tensor: 2 (over core).
Axes of the slice: x: 2, y: 2, z: 4, core: 2. Of those that a mesh axis runs over, the one named last changes fastest.
Arguments:
- inputs: bfloat16 [4096, 1024], P(('dp', 'ctx')), may hold values from -6 to 6
- lengths: int32 [4], P('dp'), may hold values from 256 to 1024, as said below
- routes: int32 [4096, 2], P(('dp', 'ctx')), may hold values from 0 to 3, as said below
- slots: int32 [4096, 2], P(('dp', 'ctx')), may hold values from -1 to 159, as said below
- first_gain: bfloat16 [1024], P(('dp', 'ctx')), may hold values from 0.5 to 1.5
- projections: bfloat16 [1024, 3, 1024], P(('dp', 'ctx'), None, 'tensor'), may hold values from -0.1875 to 0.1875
- output_weight: bfloat16 [1024, 1024], P(('dp', 'ctx'), 'tensor'), may hold values from -3 to 3
- position_bias: bfloat16 [32, 16], P(None, 'tensor'), may hold values from -3 to 3
- second_gain: bfloat16 [1024], P(('dp', 'ctx')), may hold values from 0.5 to 1.5
- router_weight: bfloat16 [1024, 4], P(('dp', 'ctx')), may hold values from -0.375 to 0.375
- gate_up: bfloat16 [4, 1024, 2, 2816], P('dp', 'ctx', None, 'tensor'), may hold values from -0.1875 to 0.1875
- down_weight: bfloat16 [4, 1024, 2816], P('dp', 'ctx', 'tensor'), may hold values from -0.4375 to 0.4375
- cotangent: bfloat16 [4096, 1024], P(('dp', 'ctx')), may hold values from -6 to 6
Outputs:
- output: bfloat16 [4096, 1024], P(('dp', 'ctx'))
- grad_inputs: float32 [4096, 1024], P(('dp', 'ctx'))
- grad_first_gain: float32 [1024], P(('dp', 'ctx'))
- grad_projections: float32 [1024, 3, 1024], P(('dp', 'ctx'), None, 'tensor')
- grad_output_weight: float32 [1024, 1024], P(('dp', 'ctx'), 'tensor')
- grad_position_bias: float32 [32, 16], P(None, 'tensor')
- grad_second_gain: float32 [1024], P(('dp', 'ctx'))
- grad_router_weight: float32 [1024, 4], P(('dp', 'ctx'))
- grad_gate_up: float32 [4, 1024, 2, 2816], P('dp', 'ctx', None, 'tensor')
- grad_down_weight: float32 [4, 1024, 2816], P('dp', 'ctx', 'tensor')
The draws below stay inside these ranges and needn't reach their ends.
Inputs may be any that keep to these rules, and one draw needn't show every extreme that they name: `lengths`: positions from a slot's length on are padding. One slot has the full 1024 in every draw. `routes`: the two experts of a position differ. slots[t, j] counts the earlier pairs of the same aligned block of 256 rows that name the same expert, in row order and then column order; it is -1 where that count reaches 160, and such a pair is dropped.
All inputs are finite; a program needn't handle non-finite values.
Results may differ from the reference program's by a relative error of at most 0.029.
Values may be sent and summed in bfloat16 or wider, within the bound.
No kernel may reach another device: no remote copies, remote signals or barrier semaphores. Data moves between devices by JAX's collectives and lax.ppermute only.
A program may use at most 192 MiB of HBM per device.

```python
import math
import jax
import jax.numpy as jnp
import numpy as np
from jax import lax

D = 1024
HEADS = 16
HD = 64
FF = 2816
BUCKETS = 32
TOK_DEV = 256
SLOT_LEN = 1024
TOKENS = 4096
EXPERTS = 4
CAP = 160
N_DP = 4
N_CTX = 4


def permute_one(row_key):
    return jax.random.permutation(row_key, TOK_DEV)


def routing_tables(key):
    groups_total = N_DP * N_CTX
    hot_per_ctx = jax.random.randint(jax.random.fold_in(key, 1), (N_CTX,), 0, EXPERTS)
    hot_expert = hot_per_ctx[jnp.arange(groups_total, dtype=jnp.int32) % N_CTX][:, None]
    takes_hot = jax.random.randint(jax.random.fold_in(key, 2), (groups_total, TOK_DEV), 0, 20) < 17
    order_keys = jax.random.split(jax.random.fold_in(key, 3), groups_total)
    ranks = jax.vmap(permute_one)(order_keys)
    include = takes_hot | (ranks <= CAP)
    offset_one = jax.random.randint(jax.random.fold_in(key, 4), (groups_total, TOK_DEV), 1, EXPERTS)
    offset_step = jax.random.randint(jax.random.fold_in(key, 5), (groups_total, TOK_DEV), 1, EXPERTS - 1)
    offset_two = 1 + (offset_one - 1 + offset_step) % (EXPERTS - 1)
    pick_one = jnp.where(include, hot_expert, (hot_expert + offset_one) % EXPERTS)
    pick_two = jnp.where(include, (hot_expert + offset_one) % EXPERTS, (hot_expert + offset_two) % EXPERTS)
    flipped = jax.random.randint(jax.random.fold_in(key, 6), (groups_total, TOK_DEV), 0, 2) == 1
    column_one = jnp.where(flipped, pick_two, pick_one)
    column_two = jnp.where(flipped, pick_one, pick_two)
    pairs = jnp.stack([column_one, column_two], axis=-1).reshape(groups_total, TOK_DEV * 2)
    one_hot = (pairs[:, :, None] == jnp.arange(EXPERTS, dtype=jnp.int32)[None, None, :]).astype(jnp.int32)
    earlier = jnp.cumsum(one_hot, axis=1) - one_hot
    counted = jnp.sum(earlier * one_hot, axis=-1)
    position_in = jnp.where(counted < CAP, counted, -1)
    return (pairs.reshape(TOKENS, 2).astype(jnp.int32), position_in.reshape(TOKENS, 2).astype(jnp.int32))


def draw_routes(key, part):
    return routing_tables(jax.random.fold_in(key, 7))[0]


def draw_slots(key, part):
    return routing_tables(jax.random.fold_in(key, 7))[1]


def draw_lengths(key, part):
    drawn = jax.random.randint(jax.random.fold_in(key, 21), (N_DP,), SLOT_LEN // 4, SLOT_LEN + 1)
    longest = jax.random.randint(jax.random.fold_in(key, 22), (), 0, N_DP)
    return jnp.where(jnp.arange(N_DP, dtype=jnp.int32) == longest, SLOT_LEN, drawn).astype(jnp.int32)


def block_levels(own_key, shape, shards, least, largest):
    gain, own = 1.0, jax.random.fold_in(own_key, 6)
    for position, blocks in shards:
        heights = jnp.exp(jax.random.uniform(jax.random.fold_in(own, position), (blocks,), jnp.float32, least / len(shards), largest / len(shards)))
        gain = gain * jnp.repeat(heights, shape[position] // blocks).reshape([-1 if axis == position else 1 for axis in range(len(shape))])
    return gain


def noise(own_key, dims, width, most, shards=(), kind=jnp.bfloat16):
    values = width * jax.random.normal(own_key, dims, jnp.float32)
    if shards:
        values = values * block_levels(own_key, dims, shards, -0.22, 0.18)
    return jnp.clip(values, -most, most).astype(kind)


def setup_inputs(seed: int = 0) -> dict:
    streams_of = jax.random.split(jax.random.key(seed), 14)
    inputs = noise(streams_of[0], (TOKENS, D), 1.0, 6.0, ((0, 16),))
    lengths = draw_lengths(jax.random.fold_in(streams_of[13], 71), 0)
    routes = draw_routes(jax.random.fold_in(streams_of[13], 71), 0)
    slots = draw_slots(jax.random.fold_in(streams_of[13], 71), 0)
    first_gain = jnp.clip(1.0 + 0.1 * jax.random.normal(streams_of[4], (D,), jnp.float32), 0.5, 1.5).astype(jnp.bfloat16)
    projections = noise(streams_of[5], (D, 3, D), D ** -0.5, 0.1875, ((0, 16), (2, 2)))
    output_weight = noise(streams_of[6], (D, D), (max(D // 256, 1)) ** -0.5, 3.0, ((0, 16), (1, 2)))
    position_bias = noise(streams_of[7], (BUCKETS, HEADS), 1.0, 3.0, ((1, 2),))
    second_gain = jnp.clip(1.0 + 0.1 * jax.random.normal(streams_of[8], (D,), jnp.float32), 0.5, 1.5).astype(jnp.bfloat16)
    router_weight = noise(streams_of[9], (D, EXPERTS), (D // 4) ** -0.5, 0.375, ((0, 16),))
    gate_up = noise(streams_of[10], (EXPERTS, D, 2, FF), D ** -0.5, 0.1875, ((0, 4), (1, 4), (3, 2)))
    down_weight = noise(streams_of[11], (EXPERTS, D, FF), (FF // 16) ** -0.5, 0.4375, ((0, 4), (1, 4), (2, 2)))
    cotangent = noise(streams_of[12], (TOKENS, D), 1.0, 6.0, ((0, 16),))
    return {"inputs": inputs, "lengths": lengths, "routes": routes, "slots": slots, "first_gain": first_gain, "projections": projections, "output_weight": output_weight, "position_bias": position_bias, "second_gain": second_gain, "router_weight": router_weight, "gate_up": gate_up, "down_weight": down_weight, "cotangent": cotangent}


BUCKET_EDGES = np.array([1, 2, 3, 4, 5, 6, 7, 8, 12, 16, 23, 32, 46, 64, 91], dtype=np.int32)
EPSILON = 1e-06
PRECISE = lax.Precision.HIGHEST

@jax.custom_vjp
def low(v):
    return lax.optimization_barrier(v.astype(jnp.bfloat16)).astype(jnp.float32)

@jax.custom_vjp
def low_back(v):
    return v

def low_keep(v):
    return (low(v), None)

def low_pass(kept, grad):
    return (grad,)

def back_keep(v):
    return (v, None)

def back_low(kept, grad):
    return (low(grad),)
low.defvjp(low_keep, low_pass)
low_back.defvjp(back_keep, back_low)

def rms_norm(values, gain_vec):
    factor = lax.rsqrt(lax.optimization_barrier(jnp.mean(values * values, axis=-1, keepdims=True)) + EPSILON)
    return values * factor * gain_vec

def bucket_of(offsets):
    magnitude = jnp.abs(offsets)
    edge_list = jnp.asarray(BUCKET_EDGES)
    counted = lax.optimization_barrier(jnp.sum((magnitude[..., None] >= edge_list).astype(jnp.int32), axis=-1))
    return counted + 16 * (offsets > 0).astype(jnp.int32)

def attend_slot(queries, keys_all, values_all, bias_values, slot_length):
    positions = jnp.arange(SLOT_LEN, dtype=jnp.int32)
    valid_key = positions < slot_length
    block_rows = math.gcd(SLOT_LEN, 512)
    factor = HD ** (-0.5)

    def one_block(operands):
        query_block, first_row = operands
        query_pos = first_row + jnp.arange(block_rows, dtype=jnp.int32)
        buckets = bucket_of(positions[None, :] - query_pos[:, None])
        bias = jnp.transpose(jnp.take(bias_values, buckets, axis=0), (2, 0, 1))
        scores = low_back(jnp.einsum('qhd,khd->hqk', query_block, keys_all, precision=PRECISE) * factor + bias)
        weights = jnp.where(valid_key[None, None, :], jnp.exp(scores), 0.0)
        totals = lax.optimization_barrier(jnp.sum(weights, axis=-1))
        summed = low_back(jnp.einsum('hqk,khd->qhd', low(weights), values_all, precision=PRECISE))
        return summed / jnp.transpose(totals)[:, :, None]
    blocks = queries.reshape(SLOT_LEN // block_rows, block_rows, HEADS, HD)
    first_rows = jnp.arange(SLOT_LEN // block_rows, dtype=jnp.int32) * block_rows
    outputs = lax.map(jax.checkpoint(one_block), (blocks, first_rows))
    return outputs.reshape(SLOT_LEN, HEADS * HD)

def run_expert(operands):
    rows_in, gate_up_one, down_one = operands
    halves = jnp.einsum('rd,dgf->rgf', rows_in, gate_up_one, precision=PRECISE)
    gate_part = low_back(halves[:, 0])
    up_part = low_back(halves[:, 1])
    hidden = low(jax.nn.gelu(gate_part, approximate=True) * up_part)
    return low_back(low(jnp.einsum('rf,df->rd', hidden, down_one, precision=PRECISE)))

def make_forward(lengths, routes, slots):
    groups_total = N_DP * N_CTX
    row_count = EXPERTS * groups_total * CAP
    token_ids = jnp.arange(TOKENS, dtype=jnp.int32)
    kept_pairs = slots >= 0
    position_in = (routes * groups_total + (token_ids // TOK_DEV)[:, None]) * CAP + slots
    target = jnp.where(kept_pairs, position_in, row_count).reshape(-1)
    sources = jnp.broadcast_to(token_ids[:, None], (TOKENS, 2)).reshape(-1)
    row_owner = jnp.full((row_count + 1,), TOKENS, dtype=jnp.int32).at[target].set(sources)[:row_count]
    pair_rows = jnp.where(kept_pairs, position_in, 0)

    def forward(inputs, first_gain, projections, output_weight, position_bias, second_gain, router_weight, gate_up, down_weight):
        normed = low(rms_norm(inputs, first_gain))
        qkv_rows = jnp.einsum('td,dgf->tgf', normed, projections, precision=PRECISE)
        queries = low_back(low(qkv_rows[:, 0])).reshape(N_DP, SLOT_LEN, HEADS, HD)
        keys_all = low_back(low(qkv_rows[:, 1])).reshape(N_DP, SLOT_LEN, HEADS, HD)
        values_all = low_back(low(qkv_rows[:, 2])).reshape(N_DP, SLOT_LEN, HEADS, HD)
        attended = jnp.concatenate([attend_slot(queries[slot_id], keys_all[slot_id], values_all[slot_id], position_bias, lengths[slot_id]) for slot_id in range(N_DP)], axis=0)
        branch = low_back(jnp.einsum('tf,df->td', low(attended), output_weight, precision=PRECISE))
        middle = inputs + branch
        second = low(rms_norm(middle, second_gain))
        logits = low_back(jnp.dot(second, router_weight, precision=PRECISE))
        router_probs = jax.nn.softmax(logits, axis=-1)
        gate_weights = jnp.where(kept_pairs, jnp.take_along_axis(router_probs, routes, axis=1), 0.0)
        padded = jnp.concatenate([second, jnp.zeros((1, D), jnp.float32)], axis=0)
        expert_rows = low_back(jnp.take(padded, row_owner, axis=0)).reshape(EXPERTS, groups_total * CAP, D)
        expert_out = lax.map(jax.checkpoint(run_expert), (expert_rows, gate_up, down_weight))
        picked = jnp.take(expert_out.reshape(row_count, D), pair_rows, axis=0)
        return middle + lax.optimization_barrier(jnp.sum(gate_weights[:, :, None] * picked, axis=1))
    return forward

def reference(inputs, lengths, routes, slots, first_gain, projections, output_weight, position_bias, second_gain, router_weight, gate_up, down_weight, cotangent):
    forward = make_forward(lengths, routes, slots)
    result, pullback = jax.vjp(forward, inputs.astype(jnp.float32), first_gain.astype(jnp.float32), projections.astype(jnp.float32), output_weight.astype(jnp.float32), position_bias.astype(jnp.float32), second_gain.astype(jnp.float32), router_weight.astype(jnp.float32), gate_up.astype(jnp.float32), down_weight.astype(jnp.float32))
    token_ids = jnp.arange(TOKENS, dtype=jnp.int32)
    visible = token_ids % SLOT_LEN < lengths[token_ids // SLOT_LEN]
    masked = jnp.where(visible[:, None], cotangent.astype(jnp.float32), 0.0)
    grad_inputs, grad_first, grad_proj, grad_out, grad_bias, grad_second, grad_router, grad_gu, grad_down = pullback(masked)
    return (result.astype(jnp.bfloat16), grad_inputs, grad_first, grad_proj, grad_out, grad_bias, grad_second, grad_router, grad_gu, grad_down)
```

```python
import functools
import math

import jax
import jax.numpy as jnp
from jax import lax
from jax.experimental import pallas as pl
from jax.experimental.pallas import tpu as pltpu
from jax.sharding import PartitionSpec as P

HD = 64


BUCKET_EDGES = [1, 2, 3, 4, 5, 6, 7, 8, 12, 16, 23, 32, 46, 64, 91]
EPSILON = 1e-06


def rms_norm(values, gain_vec):
    factor = lax.rsqrt(jnp.mean(values * values, axis=-1, keepdims=True) + EPSILON)
    return values * factor * gain_vec


def bucket_codes(offsets):
    magnitude = jnp.abs(offsets)
    counted = jnp.zeros(offsets.shape, jnp.int32)
    for edge in BUCKET_EDGES:
        counted = counted + (magnitude >= edge).astype(jnp.int32)
    return counted + 16 * (offsets > 0).astype(jnp.int32)


def gated_unit(gate_part, up_part):
    return jax.nn.gelu(gate_part, approximate=True) * up_part


def block_weights(queries, keys_block, bias_values, query_first, key_first, length, factor):
    row_count = queries.shape[0]
    col_count = keys_block.shape[0]
    bucket_total = bias_values.shape[0]
    head_count = bias_values.shape[1]
    key_pos = key_first + jnp.arange(col_count, dtype=jnp.int32)
    query_pos = query_first + jnp.arange(row_count, dtype=jnp.int32)
    buckets = bucket_codes(key_pos[None, :] - query_pos[:, None])
    bucket_ids = jnp.arange(bucket_total, dtype=jnp.int32)
    one_hot = (
        (buckets[None, :, :] == bucket_ids[:, None, None])
        .astype(jnp.bfloat16)
        .reshape(bucket_total, row_count * col_count)
    )
    table_rows = jnp.transpose(bias_values)
    table_high = table_rows.astype(jnp.bfloat16)
    table_rest = (table_rows - table_high.astype(jnp.float32)).astype(jnp.bfloat16)
    bias = jnp.dot(table_high, one_hot, preferred_element_type=jnp.float32) + jnp.dot(
        table_rest, one_hot, preferred_element_type=jnp.float32
    )
    bias = bias.reshape(head_count, row_count, col_count)
    scores = (
        jnp.einsum("qhd,khd->hqk", queries, keys_block, preferred_element_type=jnp.float32) * factor
        + bias
    )
    visible = key_pos < length
    return (one_hot, jnp.where(visible[None, None, :], jnp.exp(scores), 0.0))


def split_blocks(stacked, head_count):
    total_rows = stacked.shape[0]
    block_rows = math.gcd(total_rows, 512)
    head_size = stacked.shape[-1] // head_count
    shaped = stacked.reshape(total_rows // block_rows, block_rows, 2, head_count, head_size)
    return (shaped, block_rows)


def sweep_keys(running, stacked, first_row, queries, bias_values, query_first, length, factor):
    blocks, block_rows = split_blocks(stacked, queries.shape[1])

    def sweep_advance(state, operands):
        pair_block, number = operands
        key_first = first_row + number * block_rows
        unused, weights = block_weights(
            queries, pair_block[:, 0], bias_values, query_first, key_first, length, factor
        )
        totals = state[0] + jnp.sum(weights, axis=-1)
        summed = state[1] + jnp.einsum(
            "hqk,khd->qhd",
            weights.astype(jnp.bfloat16),
            pair_block[:, 1],
            preferred_element_type=jnp.float32,
        )
        return ((totals, summed), None)

    numbers = jnp.arange(blocks.shape[0], dtype=jnp.int32)
    running, unused = lax.scan(sweep_advance, running, (blocks, numbers))
    return running


def attention_prep(totals, attended, grad_attended):
    grad_summed = (grad_attended / jnp.transpose(totals)[:, :, None]).astype(jnp.bfloat16)
    delta = jnp.transpose(jnp.sum(grad_attended * attended, axis=-1)) / totals
    return (grad_summed, delta)


def attention_grads(queries, stacked, bias_values, query_first, length, factor, grad_summed, delta):
    head_count = queries.shape[1]
    blocks, block_rows = split_blocks(stacked, head_count)

    def attention_advance(state, operands):
        grad_queries, grad_table = state
        pair_block, number = operands
        key_first = number * block_rows
        keys_block = pair_block[:, 0]
        values_block = pair_block[:, 1]
        one_hot, weights = block_weights(
            queries, keys_block, bias_values, query_first, key_first, length, factor
        )
        inner = jnp.einsum(
            "qhd,khd->hqk", grad_summed, values_block, preferred_element_type=jnp.float32
        )
        grad_scores = (weights * (inner - delta[:, :, None])).astype(jnp.bfloat16)
        grad_queries = (
            grad_queries
            + jnp.einsum(
                "hqk,khd->qhd", grad_scores, keys_block, preferred_element_type=jnp.float32
            )
            * factor
        )
        flat_scores = grad_scores.reshape(head_count, -1)
        grad_table = grad_table + jnp.einsum(
            "hn,bn->bh", flat_scores, one_hot, preferred_element_type=jnp.float32
        )
        grad_keys = (
            jnp.einsum("hqk,qhd->khd", grad_scores, queries, preferred_element_type=jnp.float32)
            * factor
        )
        grad_values = jnp.einsum(
            "hqk,qhd->khd",
            weights.astype(jnp.bfloat16),
            grad_summed,
            preferred_element_type=jnp.float32,
        )
        return ((grad_queries, grad_table), jnp.stack([grad_keys, grad_values], axis=1))

    initial = (jnp.zeros(queries.shape, jnp.float32), jnp.zeros(bias_values.shape, jnp.float32))
    numbers = jnp.arange(blocks.shape[0], dtype=jnp.int32)
    (grad_queries, grad_table), pieces = lax.scan(attention_advance, initial, (blocks, numbers))
    pieces = pieces.reshape(stacked.shape[0], 2, -1)
    return (grad_queries, grad_table, pieces)


def on_device(
    inputs,
    lengths,
    routes,
    slots,
    first_gain,
    projections,
    output_weight,
    position_bias,
    second_gain,
    router_weight,
    gate_up,
    down_weight,
    cotangent,
):
    token_count = inputs.shape[0]
    model_width = inputs.shape[1]
    head_count = position_bias.shape[1]
    expert_count = router_weight.shape[1]
    capacity = (10 * token_count + 4 * expert_count - 1) // (4 * expert_count)
    factor = HD ** (-0.5)
    length = lengths[0]
    query_first = lax.axis_index("ctx") * token_count
    visible_rows = query_first + jnp.arange(token_count, dtype=jnp.int32) < length
    inputs_wide = inputs.astype(jnp.float32)
    bias_values = position_bias.astype(jnp.float32)
    row_total = expert_count * capacity
    kept_pairs = slots >= 0
    position_in = routes * capacity + slots
    target = jnp.where(kept_pairs, position_in, row_total).reshape(-1)
    sources = jnp.broadcast_to(
        jnp.arange(token_count, dtype=jnp.int32)[:, None], routes.shape
    ).reshape(-1)
    row_owner = (
        jnp.full((row_total + 1,), token_count, jnp.int32).at[target].set(sources)[:row_total]
    )
    pair_rows = jnp.where(kept_pairs, position_in, 0)

    def to_rows(values):
        padded = jnp.concatenate([values, jnp.zeros((1, values.shape[1]), values.dtype)], axis=0)
        return jnp.take(padded, row_owner, axis=0).reshape(expert_count, capacity, values.shape[1])

    def gather_dense():
        return (
            lax.all_gather(projections, ("dp", "ctx"), axis=0, tiled=True),
            lax.all_gather(output_weight, ("dp", "ctx"), axis=0, tiled=True),
            lax.all_gather(first_gain, ("dp", "ctx"), axis=0, tiled=True),
            lax.all_gather(second_gain, ("dp", "ctx"), axis=0, tiled=True),
            lax.all_gather(router_weight, ("dp", "ctx"), axis=0, tiled=True),
        )

    def gather_experts():
        return (
            lax.all_gather(gate_up, "ctx", axis=1, tiled=True),
            lax.all_gather(down_weight, "ctx", axis=1, tiled=True),
        )

    def across_tensor(values):
        return lax.psum(values.astype(jnp.bfloat16), "tensor").astype(jnp.float32)

    def to_experts(values):
        return lax.all_to_all(values, "dp", split_axis=0, concat_axis=0, tiled=True)

    def from_experts(values):
        return lax.all_to_all(values, "dp", split_axis=0, concat_axis=0, tiled=True)

    def project(weights_qkv, gain_one):
        normed = rms_norm(inputs_wide, gain_one.astype(jnp.float32)).astype(jnp.bfloat16)
        qkv_rows = jnp.einsum(
            "td,dgf->tgf", normed, weights_qkv, preferred_element_type=jnp.float32
        ).astype(jnp.bfloat16)
        return (normed, qkv_rows)

    def empty_carry():
        return (
            jnp.zeros((head_count, token_count), jnp.float32),
            jnp.zeros((token_count, head_count, HD), jnp.float32),
        )

    def finish_attention(carried, weight_out):
        attended = carried[1] / jnp.transpose(carried[0])[:, :, None]
        attended_low = attended.reshape(token_count, -1).astype(jnp.bfloat16)
        middle = inputs_wide + across_tensor(
            jnp.einsum("tf,df->td", attended_low, weight_out, preferred_element_type=jnp.float32)
        )
        return (attended, attended_low, middle)

    def route_tokens(middle, gain_two, weight_router):
        second = rms_norm(middle, gain_two.astype(jnp.float32)).astype(jnp.bfloat16)
        logits = jnp.dot(second, weight_router, preferred_element_type=jnp.float32)
        router_probs = jax.nn.softmax(logits, axis=-1)
        gate_weights = jnp.where(kept_pairs, jnp.take_along_axis(router_probs, routes, axis=1), 0.0)
        return (second, router_probs, gate_weights)

    def expert_forward(received, weight_gu, weight_down):
        local_count = weight_gu.shape[0]
        grid_rows = received.reshape(-1, local_count, capacity, model_width)
        halves = jnp.einsum(
            "secd,edgf->secgf", grid_rows, weight_gu, preferred_element_type=jnp.float32
        )
        hidden = gated_unit(halves[..., 0, :], halves[..., 1, :]).astype(jnp.bfloat16)
        partial_out = jnp.einsum(
            "secf,edf->secd", hidden, weight_down, preferred_element_type=jnp.float32
        )
        return (grid_rows, halves, hidden, partial_out)

    dense = gather_dense()
    expert_set = gather_experts()
    normed, qkv_rows = project(dense[0], dense[2])
    queries = qkv_rows[:, 0].reshape(token_count, head_count, HD)
    carried = sweep_keys(
        empty_carry(),
        lax.all_gather(qkv_rows[:, 1:], "ctx", axis=0, tiled=True),
        jnp.int32(0),
        queries,
        bias_values,
        query_first,
        length,
        factor,
    )
    attended, attended_low, middle = finish_attention(carried, dense[1])
    second, router_probs, gate_weights = route_tokens(middle, dense[3], dense[4])
    received = to_experts(to_rows(second))
    grid_rows, halves, hidden, partial_out = expert_forward(received, expert_set[0], expert_set[1])
    summed_out = across_tensor(partial_out).astype(jnp.bfloat16).reshape(-1, capacity, model_width)
    returned = from_experts(summed_out).reshape(row_total, model_width)
    output = middle + jnp.sum(
        gate_weights[:, :, None] * jnp.take(returned, pair_rows, axis=0).astype(jnp.float32), axis=1
    )
    dense = gather_dense()
    expert_set = gather_experts()
    normed, qkv_rows = project(dense[0], dense[2])
    queries = qkv_rows[:, 0].reshape(token_count, head_count, HD)
    whole = lax.all_gather(qkv_rows[:, 1:], "ctx", axis=0, tiled=True)
    carried = sweep_keys(empty_carry(), whole, 0, queries, bias_values, query_first, length, factor)
    attended, attended_low, middle = finish_attention(carried, dense[1])
    second, router_probs, gate_weights = route_tokens(middle, dense[3], dense[4])
    grad_output = jnp.where(visible_rows[:, None], cotangent.astype(jnp.float32), 0.0)
    gate_rows = (
        jnp.zeros((row_total + 1,), jnp.float32)
        .at[target]
        .set(gate_weights.reshape(-1))[:row_total]
        .reshape(expert_count, capacity)
    )
    grad_rows = (to_rows(grad_output) * gate_rows[:, :, None]).astype(jnp.bfloat16)
    arrived = to_experts(jnp.stack([to_rows(second), grad_rows], axis=1))
    grid_rows, halves, hidden, partial_out = expert_forward(
        arrived[:, 0], expert_set[0], expert_set[1]
    )
    grad_grid = arrived[:, 1].reshape(grid_rows.shape)
    grad_hidden = jnp.einsum(
        "secd,edf->secf", grad_grid, expert_set[1], preferred_element_type=jnp.float32
    )
    grad_down = jnp.einsum("secf,secd->edf", hidden, grad_grid, preferred_element_type=jnp.float32)
    unused, unit_back = jax.vjp(gated_unit, halves[..., 0, :], halves[..., 1, :])
    grad_gate, grad_up = unit_back(grad_hidden)
    grad_halves = jnp.stack([grad_gate, grad_up], axis=-2).astype(jnp.bfloat16)
    grad_gu = jnp.einsum(
        "secd,secgf->edgf", grid_rows, grad_halves, preferred_element_type=jnp.float32
    )
    grad_in = jnp.einsum(
        "secgf,edgf->secd", grad_halves, expert_set[0], preferred_element_type=jnp.float32
    )
    grad_gu, grad_down, grad_in = (grad_gu, grad_down, grad_in)
    both_sums = across_tensor(jnp.stack([partial_out, grad_in], axis=0)).astype(jnp.bfloat16)
    going_back = jnp.stack(
        [
            both_sums[0].reshape(-1, capacity, model_width),
            both_sums[1].reshape(-1, capacity, model_width),
        ],
        axis=1,
    )
    came_back = from_experts(going_back)
    returned = came_back[:, 0].reshape(row_total, model_width)
    grad_second_rows = came_back[:, 1].reshape(row_total, model_width)
    picked = jnp.take(returned, pair_rows, axis=0).astype(jnp.float32)
    grad_gates = jnp.where(kept_pairs, jnp.sum(picked * grad_output[:, None, :], axis=-1), 0.0)
    expert_ids = jnp.arange(expert_count, dtype=jnp.int32)
    grad_probs = jnp.sum(
        jnp.where(routes[:, :, None] == expert_ids[None, None, :], grad_gates[:, :, None], 0.0),
        axis=1,
    )
    grad_logits = (
        router_probs * (grad_probs - jnp.sum(router_probs * grad_probs, axis=-1, keepdims=True))
    ).astype(jnp.bfloat16)
    grad_router = jnp.einsum("td,te->de", second, grad_logits, preferred_element_type=jnp.float32)
    from_rows = jnp.take(grad_second_rows, pair_rows, axis=0).astype(jnp.float32)
    grad_second = jnp.sum(jnp.where(kept_pairs[:, :, None], from_rows, 0.0), axis=1) + jnp.einsum(
        "te,de->td", grad_logits, dense[4], preferred_element_type=jnp.float32
    )
    unused, second_back = jax.vjp(rms_norm, middle, dense[3].astype(jnp.float32))
    grad_middle_norm, grad_gain_two = second_back(grad_second)
    grad_middle = grad_output + grad_middle_norm
    grad_branch = grad_middle.astype(jnp.bfloat16)
    grad_out_weight = jnp.einsum(
        "td,tf->df", grad_branch, attended_low, preferred_element_type=jnp.float32
    )
    grad_attended = jnp.einsum(
        "td,df->tf", grad_branch, dense[1], preferred_element_type=jnp.float32
    ).reshape(token_count, head_count, HD)
    grad_summed, delta = attention_prep(carried[0], attended, grad_attended)
    grad_queries, grad_table, key_terms = attention_grads(
        queries, whole, bias_values, query_first, length, factor, grad_summed, delta
    )
    grad_pairs = lax.psum_scatter(
        key_terms.astype(jnp.bfloat16), "ctx", scatter_dimension=0, tiled=True
    )
    grad_qkv = jnp.concatenate(
        [grad_queries.reshape(token_count, 1, -1).astype(jnp.bfloat16), grad_pairs], axis=1
    )
    grad_proj = jnp.einsum("td,tgf->dgf", normed, grad_qkv, preferred_element_type=jnp.float32)
    grad_normed = across_tensor(
        jnp.einsum("tgf,dgf->td", grad_qkv, dense[0], preferred_element_type=jnp.float32)
    )
    unused, first_back = jax.vjp(rms_norm, inputs_wide, dense[2].astype(jnp.float32))
    grad_input_norm, grad_gain_one = first_back(grad_normed)
    grad_inputs = grad_middle + grad_input_norm
    dense_sums = (
        lax.psum_scatter(grad_proj, ("dp", "ctx"), scatter_dimension=0, tiled=True),
        lax.psum_scatter(grad_out_weight, ("dp", "ctx"), scatter_dimension=0, tiled=True),
        lax.psum_scatter(grad_gain_one, ("dp", "ctx"), scatter_dimension=0, tiled=True),
        lax.psum_scatter(grad_gain_two, ("dp", "ctx"), scatter_dimension=0, tiled=True),
        lax.psum_scatter(grad_router, ("dp", "ctx"), scatter_dimension=0, tiled=True),
    )
    expert_sums = (
        lax.psum_scatter(
            grad_gu.astype(jnp.bfloat16), "ctx", scatter_dimension=1, tiled=True
        ).astype(jnp.float32),
        lax.psum_scatter(
            grad_down.astype(jnp.bfloat16), "ctx", scatter_dimension=1, tiled=True
        ).astype(jnp.float32),
    )
    bias_sum = lax.psum(grad_table, ("dp", "ctx"))
    return (
        output.astype(jnp.bfloat16),
        grad_inputs,
        dense_sums[2],
        dense_sums[0],
        dense_sums[1],
        bias_sum,
        dense_sums[3],
        dense_sums[4],
        expert_sums[0],
        expert_sums[1],
    )


LANES = 128
QB = 256


def bias_tiles_kernel(table_ref, out_ref):
    head = pl.program_id(0)

    def entry(bucket):
        return table_ref[bucket * 2 + head]

    half = len(BUCKET_EDGES) + 1
    out_ref[0, 0] = jnp.full((QB, QB), entry(half - 1), jnp.float32)
    out_ref[0, 4] = jnp.full((QB, QB), entry(2 * half - 1), jnp.float32)
    chunk = 32
    for delta in (-1, 0, 1):

        def rows(step, carry, delta=delta):
            first = pl.multiple_of(step * chunk, chunk)
            i = first + lax.broadcasted_iota(jnp.int32, (chunk, QB), 0)
            j = lax.broadcasted_iota(jnp.int32, (chunk, QB), 1)
            offset = j - i + QB * delta
            magnitude = jnp.abs(offset)
            value = jnp.full((chunk, QB), entry(0), jnp.float32)
            if delta <= 0:
                for number, edge in enumerate(BUCKET_EDGES):
                    value = jnp.where(magnitude >= edge, entry(number + 1), value)
            if delta >= 0:
                right = jnp.full((chunk, QB), entry(half), jnp.float32)
                for number, edge in enumerate(BUCKET_EDGES):
                    right = jnp.where(magnitude >= edge, entry(half + number + 1), right)
                value = jnp.where(offset > 0, right, value)
            out_ref[0, delta + 2, pl.ds(first, chunk), :] = value
            return carry

        lax.fori_loop(0, QB // chunk, rows, 0)


def bias_tiles(table):
    return pl.pallas_call(
        bias_tiles_kernel,
        grid=(2,),
        out_shape=jax.ShapeDtypeStruct((2, 5, QB, QB), jnp.float32),
        in_specs=[pl.BlockSpec(memory_space=pltpu.SMEM)],
        out_specs=pl.BlockSpec((1, 5, QB, QB), lambda h: (h, 0, 0, 0)),
        cost_estimate=pl.CostEstimate(flops=2 * 5 * QB * QB * 40, bytes_accessed=2 * 5 * QB * QB * 4, transcendentals=0),
    )(table.reshape(-1))


def lane_masks():
    lane = lax.broadcasted_iota(jnp.int32, (1, LANES), 1)
    return [lane < HD, lane >= HD]


NT = (((1,), (1,)), ((), ()))
TN = (((0,), (0,)), ((), ()))


def tile_weights(q_head, keys, bias, key_first, length):
    scores = lax.dot_general(q_head, keys, NT, preferred_element_type=jnp.float32) + bias
    key_pos = key_first + lax.broadcasted_iota(jnp.int32, (1, QB), 1)
    return jnp.where(key_pos < length, jnp.exp(scores), 0.0)


def attention_fwd_kernel(info_ref, q_ref, k_ref, v_ref, bias_ref, low_ref, wide_ref, inverse_ref):
    block = pl.program_id(0)
    count = pl.num_programs(0)
    blocks = k_ref.shape[0] // QB
    length = info_ref[blocks]
    mine = info_ref[block]
    masks = lane_masks()
    sums, totals = [], []
    for head in range(2):
        q_head = jnp.where(masks[head], q_ref[...], 0.0) * jnp.bfloat16(HD ** (-0.5))
        acc = jnp.zeros((QB, LANES), jnp.float32)
        total = jnp.zeros((QB, 1), jnp.float32)
        for other in range(blocks):
            there = info_ref[other]
            kind = jnp.clip(there - mine, -2, 2) + 2
            rows = pl.ds(other * QB, QB)
            weights = tile_weights(q_head, k_ref[rows, :], bias_ref[head, kind], there * QB, length)
            total = total + jnp.sum(weights, axis=-1, keepdims=True)
            acc = acc + jnp.dot(weights.astype(jnp.bfloat16), v_ref[rows, :], preferred_element_type=jnp.float32)
        sums.append(acc)
        totals.append(1.0 / total)
    inverse = jnp.where(masks[0], totals[0], totals[1])
    wide = jnp.where(masks[0], sums[0], sums[1]) * inverse
    wide_ref[...] = wide
    low_ref[...] = wide.astype(jnp.bfloat16)
    inverse_ref[...] = inverse


def attention_fwd(info, qkv, bias):
    rows = qkv.shape[0]
    row_block = pl.BlockSpec((QB, LANES), lambda i: (i, 0))
    full = lambda col: pl.BlockSpec((rows, LANES), lambda i: (0, col))
    return pl.pallas_call(
        attention_fwd_kernel,
        grid=(rows // QB,),
        out_shape=(
            jax.ShapeDtypeStruct((rows, LANES), jnp.bfloat16),
            jax.ShapeDtypeStruct((rows, LANES), jnp.float32),
            jax.ShapeDtypeStruct((rows, LANES), jnp.float32),
        ),
        in_specs=[
            pl.BlockSpec(memory_space=pltpu.SMEM),
            row_block,
            full(1),
            full(2),
            pl.BlockSpec((2, 5, QB, QB), lambda i: (0, 0, 0, 0)),
        ],
        out_specs=(row_block, row_block, row_block),
        cost_estimate=pl.CostEstimate(flops=16 * rows * rows * LANES, bytes_accessed=5 * 2 * QB * QB * 4 + rows * LANES * 16, transcendentals=2 * rows * rows),
    )(info, qkv, qkv, qkv, bias)


def attention_bwd_kernel(info_ref, q_ref, k_ref, v_ref, bias_ref, grad_ref, wide_ref, inverse_ref, dq_ref, dk_ref, dv_ref, table_ref, acc_k, acc_v, acc_t):
    block = pl.program_id(0)
    blocks = k_ref.shape[0] // QB
    length = info_ref[blocks]
    mine = info_ref[block]
    masks = lane_masks()

    @pl.when(block == 0)
    def _():
        acc_k[...] = jnp.zeros_like(acc_k)
        acc_v[...] = jnp.zeros_like(acc_v)
        acc_t[...] = jnp.zeros_like(acc_t)

    grad = grad_ref[...].astype(jnp.float32)
    inverse = inverse_ref[...]
    grad_summed = (grad * inverse).astype(jnp.bfloat16)
    products = grad * wide_ref[...] * inverse
    scaled = q_ref[...] * jnp.bfloat16(HD ** (-0.5))
    dq = jnp.zeros((QB, LANES), jnp.float32)
    for head in range(2):
        mask = masks[head]
        delta = jnp.sum(jnp.where(mask, products, 0.0), axis=-1, keepdims=True)
        q_head = jnp.where(mask, scaled, 0.0)
        g_head = jnp.where(mask, grad_summed, 0.0)
        for other in range(blocks):
            there = info_ref[other]
            kind = jnp.clip(there - mine, -2, 2) + 2
            rows = pl.ds(other * QB, QB)
            keys = k_ref[rows, :]
            weights = tile_weights(q_head, keys, bias_ref[head, kind], there * QB, length)
            inner = lax.dot_general(g_head, v_ref[rows, :], NT, preferred_element_type=jnp.float32)
            scores = (weights * (inner - delta)).astype(jnp.bfloat16)
            acc_t[head, kind] += scores.astype(jnp.float32)
            k_head = jnp.where(mask, keys, 0.0)
            dq = dq + jnp.dot(scores, k_head, preferred_element_type=jnp.float32)
            acc_k[rows, :] += lax.dot_general(scores, q_head, TN, preferred_element_type=jnp.float32)
            acc_v[rows, :] += lax.dot_general(weights.astype(jnp.bfloat16), g_head, TN, preferred_element_type=jnp.float32)
    dq_ref[...] = (dq * HD ** (-0.5)).astype(jnp.bfloat16)

    @pl.when(block == pl.num_programs(0) - 1)
    def _():
        dk_ref[...] = acc_k[...].astype(jnp.bfloat16)
        dv_ref[...] = acc_v[...].astype(jnp.bfloat16)
        half = len(BUCKET_EDGES) + 1
        low, high = slice(0, LANES), slice(LANES, QB)
        ends = list(BUCKET_EDGES) + [1 << 20]
        starts = [0] + list(BUCKET_EDGES)
        i = lax.broadcasted_iota(jnp.int32, (LANES, LANES), 0)
        j = lax.broadcasted_iota(jnp.int32, (LANES, LANES), 1)
        for head in range(2):
            tile = lambda kind, rows, cols: acc_t[head, kind, rows, cols]
            near = {
                -1: tile(2, high, low) + tile(1, low, high),
                0: tile(2, low, low) + tile(2, high, high),
                1: tile(2, low, high) + tile(3, high, low),
            }
            left = tile(1, low, low) + tile(1, high, low) + tile(1, high, high)
            left = left + tile(0, low, low) + tile(0, low, high) + tile(0, high, low) + tile(0, high, high)
            right = tile(3, low, low) + tile(3, low, high) + tile(3, high, high)
            right = right + tile(4, low, low) + tile(4, low, high) + tile(4, high, low) + tile(4, high, high)
            line = lambda part: jnp.sum(part, axis=0, keepdims=True)
            for number in range(2 * half):
                bucket = number % half
                total = jnp.zeros((1, LANES), jnp.float32)
                if number == half - 1:
                    total = total + line(left)
                if number == 2 * half - 1:
                    total = total + line(right)
                for delta, values in near.items():
                    offset = j - i + LANES * delta
                    if number < half:
                        if delta == 1:
                            continue
                        keep = (-offset >= starts[bucket]) & (-offset < ends[bucket])
                    else:
                        if delta == -1 or bucket == 0:
                            continue
                        keep = (offset >= starts[bucket]) & (offset < ends[bucket])
                    total = total + line(jnp.where(keep, values, 0.0))
                table_ref[head, number : number + 1, :] = total


def attention_bwd(info, qkv, bias, grad, wide, inverse):
    rows = qkv.shape[0]
    row_block = pl.BlockSpec((QB, LANES), lambda i: (i, 0))
    full = lambda col: pl.BlockSpec((rows, LANES), lambda i: (0, col))
    return pl.pallas_call(
        attention_bwd_kernel,
        grid=(rows // QB,),
        out_shape=(
            jax.ShapeDtypeStruct((rows, LANES), jnp.bfloat16),
            jax.ShapeDtypeStruct((rows, LANES), jnp.bfloat16),
            jax.ShapeDtypeStruct((rows, LANES), jnp.bfloat16),
            jax.ShapeDtypeStruct((2, 32, LANES), jnp.float32),
        ),
        in_specs=[
            pl.BlockSpec(memory_space=pltpu.SMEM),
            row_block,
            full(1),
            full(2),
            pl.BlockSpec((2, 5, QB, QB), lambda i: (0, 0, 0, 0)),
            row_block,
            row_block,
            row_block,
        ],
        out_specs=(row_block, full(0), full(0), pl.BlockSpec((2, 32, LANES), lambda i: (0, 0, 0))),
        scratch_shapes=[
            pltpu.VMEM((rows, LANES), jnp.float32),
            pltpu.VMEM((rows, LANES), jnp.float32),
            pltpu.VMEM((2, 5, QB, QB), jnp.float32),
        ],
        cost_estimate=pl.CostEstimate(flops=36 * rows * rows * LANES, bytes_accessed=5 * 2 * QB * QB * 4 + rows * LANES * 16, transcendentals=2 * rows * rows),
    )(info, qkv, qkv, qkv, bias, grad, wide, inverse)


def xor_order(blocks, index):
    blocks = list(blocks)
    bit = 1
    while bit < len(blocks):
        odd = (index & bit) != 0
        blocks = [jnp.where(odd, blocks[k ^ bit], blocks[k]) for k in range(len(blocks))]
        bit *= 2
    return blocks


def on_device_fast(sizes, inputs, lengths, routes, slots, first_gain, projections, output_weight, position_bias, second_gain, router_weight, gate_up, down_weight, cotangent):
    n_dp, n_ctx = sizes["dp"], sizes["ctx"]
    tokens, width = inputs.shape
    heads = position_bias.shape[1]
    experts = router_weight.shape[1]
    hidden_units = gate_up.shape[3]
    capacity = (10 * tokens + 4 * experts - 1) // (4 * experts)
    shard = first_gain.shape[0]
    group = heads * HD // n_ctx
    half_rows, half = tokens // 2, width // 2
    quarter = width // n_ctx
    d, c, t = (lax.axis_index(name) for name in ("dp", "ctx", "tensor"))
    f32, bf16 = jnp.float32, jnp.bfloat16

    def send(values, axis, m):
        return lax.ppermute(values, axis, [(i, i ^ m) for i in range(sizes[axis])])

    def partner(values):
        return send(values, "tensor", 1)

    ctx_peers, dp_peers = range(1, n_ctx), range(1, n_dp)

    def pair_sum(parts):
        parts = list(parts)
        while len(parts) > 1:
            parts = [parts[k] + parts[k + 1] for k in range(0, len(parts), 2)]
        return parts[0]

    def by_core(mine, other, axis):
        first = jnp.where(t == 0, mine, other)
        second = jnp.where(t == 0, other, mine)
        return jnp.concatenate([first, second], axis=axis)

    def half_of(values, which, axis):
        size = values.shape[axis] // 2
        return lax.dynamic_slice_in_dim(values, which * size, size, axis)

    mine = jnp.stack([send(half_of(inputs, t, 0), "ctx", m) for m in ctx_peers])
    gathered = by_core(mine, partner(mine), 1)
    slot_inputs = jnp.concatenate([inputs[None], gathered]).reshape(n_ctx * tokens, width)

    small = jnp.concatenate([first_gain, second_gain, router_weight.reshape(-1)])
    small_rows = -(-small.shape[0] // LANES)
    small_pad = -(-small_rows // 16) * 16
    small = jnp.pad(small, (0, small_pad * LANES - small.shape[0])).reshape(small_pad, LANES)
    out_cut = jnp.transpose(output_weight.reshape(shard, n_ctx, group), (1, 0, 2)).reshape(n_ctx * shard, group)
    columns = projections.reshape(shard, 3, n_ctx, group)

    def payload(m):
        cut = lax.dynamic_index_in_dim(columns, c ^ m, 2, keepdims=False)
        return jnp.concatenate([jnp.transpose(cut, (1, 0, 2)).reshape(3 * shard, group), small, out_cut])

    pieces = xor_order([payload(0)] + [send(payload(m), "ctx", m) for m in ctx_peers], c)
    head_rows = 3 * shard + small_pad
    first_part = jnp.stack([p[:head_rows] for p in pieces])
    out_part = jnp.stack([p[head_rows:] for p in pieces])
    first_all = jnp.stack(xor_order([first_part] + [send(first_part, "dp", m) for m in dp_peers], d))
    weight_rows = first_all[:, :, : 3 * shard].reshape(n_dp, n_ctx, 3, shard, group)
    w_qkv = jnp.transpose(weight_rows, (0, 1, 3, 2, 4)).reshape(width, 3 * group)
    small_all = first_all[:, :, 3 * shard : 3 * shard + small_rows].reshape(n_dp * n_ctx, -1)
    gain_one = small_all[:, :shard].reshape(width).astype(f32)
    gain_two = small_all[:, shard : 2 * shard].reshape(width).astype(f32)
    w_router = small_all[:, 2 * shard : (2 + experts) * shard].reshape(width, experts)
    out_all = jnp.stack(xor_order([out_part] + [send(out_part, "dp", m) for m in dp_peers], d))
    w_out = jnp.transpose(out_all.reshape(n_dp, n_ctx, n_ctx, shard, group), (0, 1, 3, 2, 4)).reshape(width, n_ctx * group)

    own = jnp.concatenate([gate_up[0].reshape(quarter, 2 * hidden_units), down_weight[0]], axis=1)
    top, bottom = own[: quarter // 2], own[quarter // 2 :]
    top1, bottom2 = send(top, "ctx", 1), send(bottom, "ctx", 2)
    top2, bottom1 = send(top, "ctx", 2), send(bottom, "ctx", 1)
    top3, bottom3 = send(top1, "ctx", 2), send(bottom2, "ctx", 1)
    w_experts = jnp.concatenate([own, top1, bottom1, top2, bottom2, top3, bottom3])
    w_gate, w_up, w_down = (w_experts[:, k * hidden_units : (k + 1) * hidden_units] for k in range(3))

    def inverse_rms(values):
        return lax.rsqrt(jnp.mean(values * values, axis=-1, keepdims=True) + EPSILON)

    slot_wide = slot_inputs.astype(f32)
    slot_factor = inverse_rms(slot_wide)
    normed = (slot_wide * slot_factor * gain_one).astype(bf16)
    qkv = jnp.dot(normed, w_qkv, preferred_element_type=f32).astype(bf16)
    places = c ^ jnp.arange(n_ctx, dtype=jnp.int32)
    info = jnp.concatenate([places, lengths]).astype(jnp.int32)
    own_heads = lax.dynamic_slice_in_dim(position_bias, c * 2, 2, 1).astype(f32)
    tiles = bias_tiles(own_heads)
    low, wide, inverse = attention_fwd(info, qkv, tiles)

    low4 = low.reshape(n_ctx, tokens, group)
    attended = jnp.concatenate(xor_order([low4[0]] + [send(low4[m], "ctx", m) for m in ctx_peers], c), axis=1)
    branch = lax.dot_general(attended, w_out, NT, preferred_element_type=f32).astype(bf16)
    inputs_wide = inputs.astype(f32)
    middle = inputs_wide + (branch.astype(f32) + partner(branch).astype(f32))

    factor_two = inverse_rms(middle)
    second = (middle * factor_two * gain_two).astype(bf16)
    probs = jax.nn.softmax(jnp.dot(second, w_router, preferred_element_type=f32), axis=-1)
    kept = slots >= 0
    expert_ids = jnp.arange(experts, dtype=jnp.int32)
    choice = routes[:, :, None] == expert_ids
    gates = jnp.where(kept, jnp.sum(jnp.where(choice, probs[:, None, :], 0.0), axis=-1), 0.0)
    row_total = experts * capacity
    target = jnp.where(kept, (routes ^ d) * capacity + slots, -1)
    row_ids = jnp.arange(row_total, dtype=jnp.int32)
    hit = [target[:, j][None, :] == row_ids[:, None] for j in range(2)]
    place = (hit[0] | hit[1]).astype(bf16)
    row_gates = jnp.sum(jnp.where(hit[0], gates[:, 0][None, :], 0.0) + jnp.where(hit[1], gates[:, 1][None, :], 0.0), axis=1, keepdims=True)
    query_first = c * tokens
    visible = query_first + jnp.arange(tokens, dtype=jnp.int32) < lengths[0]
    grad_low = jnp.where(visible[:, None], cotangent, 0)
    grad_output = grad_low.astype(f32)

    def shuffle(values):
        return jnp.concatenate(xor_order([values[:, k * quarter : (k + 1) * quarter] for k in range(n_ctx)], c), axis=1)

    def to_experts(rows):
        cut = half_of(rows, t, 1).reshape(experts, capacity, half)
        arrived = jnp.stack([send(cut[m], "dp", m) for m in dp_peers]).reshape(-1, half)
        rest = by_core(arrived, partner(arrived), 1)
        return jnp.concatenate([rows[:capacity], rest])

    def from_experts(part):
        low_part = part.astype(bf16)
        kept_half, gone_half = half_of(low_part, t, 1), half_of(low_part, 1 - t, 1)
        summed = (kept_half.astype(f32) + partner(gone_half).astype(f32)).astype(bf16).reshape(experts, capacity, half)
        arrived = jnp.stack([summed[0]] + [send(summed[m], "dp", m) for m in dp_peers]).reshape(-1, half)
        return by_core(arrived, partner(arrived), 1)

    rows_in = to_experts(jnp.dot(place, shuffle(second), preferred_element_type=f32).astype(bf16))
    rows_grad = to_experts((jnp.dot(place, shuffle(grad_low), preferred_element_type=f32) * row_gates).astype(bf16))

    gate_part = jnp.dot(rows_in, w_gate, preferred_element_type=f32)
    up_part = jnp.dot(rows_in, w_up, preferred_element_type=f32)
    hidden, unit_back = jax.vjp(gated_unit, gate_part, up_part)
    hidden = hidden.astype(bf16)
    returned = from_experts(lax.dot_general(hidden, w_down, NT, preferred_element_type=f32))
    grad_hidden = jnp.dot(rows_grad, w_down, preferred_element_type=f32)
    grad_gate, grad_up = unit_back(grad_hidden)
    grad_halves = jnp.concatenate([grad_gate, grad_up], axis=1).astype(bf16)
    grad_rows = from_experts(
        lax.dot_general(grad_halves, w_experts[:, : 2 * hidden_units], NT, preferred_element_type=f32)
    )
    grad_w = jnp.concatenate(
        [
            lax.dot_general(rows_in, grad_halves, TN, preferred_element_type=f32).astype(bf16),
            lax.dot_general(rows_grad, hidden, TN, preferred_element_type=f32).astype(bf16),
        ],
        axis=1,
    ).reshape(n_ctx, 2, quarter // 2, 3 * hidden_units)
    top_back = send(grad_w[1::2, 0], "ctx", 1)
    bottom_back = send(grad_w[2:, 1], "ctx", 2)
    top_keep = grad_w[0::2, 0].astype(f32) + top_back.astype(f32)
    bottom_keep = grad_w[:2, 1].astype(f32) + bottom_back.astype(f32)
    top_sum = top_keep[0] + send(top_keep[1].astype(bf16), "ctx", 2).astype(f32)
    bottom_sum = bottom_keep[0] + send(bottom_keep[1].astype(bf16), "ctx", 1).astype(f32)
    grad_experts = jnp.concatenate([top_sum, bottom_sum])
    grad_gate_up = grad_experts[:, : 2 * hidden_units].reshape(1, quarter, 2, hidden_units)
    grad_down = grad_experts[:, 2 * hidden_units :][None]

    picks = [jnp.transpose(h).astype(bf16) for h in hit]
    picked = [shuffle(jnp.dot(p, returned, preferred_element_type=f32)) for p in picks]
    output = middle + (gates[:, :1] * picked[0] + gates[:, 1:] * picked[1])
    grad_gates = jnp.stack([jnp.sum(p * grad_output, axis=-1) for p in picked], axis=1)
    grad_gates = jnp.where(kept, grad_gates, 0.0)
    grad_probs = jnp.sum(jnp.where(choice, grad_gates[:, :, None], 0.0), axis=1)
    grad_logits = (probs * (grad_probs - jnp.sum(probs * grad_probs, axis=-1, keepdims=True))).astype(bf16)
    grad_router = lax.dot_general(second, grad_logits, TN, preferred_element_type=f32)
    grad_second = shuffle(jnp.dot(picks[0] + picks[1], grad_rows, preferred_element_type=f32)) + lax.dot_general(
        grad_logits, w_router, NT, preferred_element_type=f32
    )
    grad_gain_two = jnp.sum(grad_second * middle * factor_two, axis=0)
    gained = grad_second * gain_two
    grad_middle = (
        grad_output + factor_two * gained - middle * (factor_two**3 * jnp.mean(middle * gained, axis=-1, keepdims=True))
    )
    grad_branch = grad_middle.astype(bf16)
    grad_attended = jnp.dot(grad_branch, w_out, preferred_element_type=f32).astype(bf16)
    cuts = xor_order([grad_attended[:, k * group : (k + 1) * group] for k in range(n_ctx)], c)
    grad_heads = jnp.concatenate([cuts[0]] + [send(cuts[m], "ctx", m) for m in ctx_peers])

    grad_out = lax.dot_general(grad_branch, attended, TN, preferred_element_type=f32).astype(bf16)
    blocks = xor_order([grad_out[k * quarter : (k + 1) * quarter] for k in range(n_dp)], d)
    blocks = pair_sum([b.astype(f32) for b in [blocks[0]] + [send(blocks[m], "dp", m) for m in dp_peers]]).astype(bf16)
    blocks = xor_order([blocks[k * shard : (k + 1) * shard] for k in range(n_ctx)], c)
    grad_output_weight = pair_sum([b.astype(f32) for b in [blocks[0]] + [send(blocks[m], "ctx", m) for m in ctx_peers]])

    dq, dk, dv, table = attention_bwd(info, qkv, tiles, grad_heads, wide, inverse)
    grad_qkv = jnp.concatenate([dq, dk, dv], axis=1)
    table_part = jnp.sum(table, axis=-1)
    part = lax.dot_general(grad_qkv, w_qkv, NT, preferred_element_type=f32)
    gain_part = jnp.sum(part * (slot_wide * slot_factor), axis=0).astype(bf16)
    part = part.astype(bf16)
    extra = jnp.pad(gain_part.reshape(2, half), ((0, 14), (0, 0)))
    came = partner(jnp.concatenate([half_of(part, 1 - t, 1), extra]))
    grad_gain_one = gain_part.astype(f32) + came[-16:-14].reshape(width).astype(f32)
    core_sum = (half_of(part, t, 1).astype(f32) + came[:-16].astype(f32)).astype(bf16).reshape(n_ctx, tokens, half)
    own_half = pair_sum([b.astype(f32) for b in [core_sum[0]] + [send(core_sum[m], "ctx", m) for m in ctx_peers]])
    grad_normed = by_core(own_half, partner(own_half), 1)
    factor_one = slot_factor[:tokens]
    gained = grad_normed * gain_one
    grad_inputs = (
        grad_middle
        + factor_one * gained
        - inputs_wide * (factor_one**3 * jnp.mean(inputs_wide * gained, axis=-1, keepdims=True))
    )

    cols = 3 * group
    grad_proj = lax.dot_general(normed, grad_qkv, TN, preferred_element_type=f32).astype(bf16)
    small_grads = jnp.concatenate(
        [
            grad_gain_one.reshape(n_dp, n_ctx, shard),
            grad_gain_two.reshape(n_dp, n_ctx, shard),
            grad_router.reshape(n_dp, n_ctx, shard * experts),
        ],
        axis=2,
    ).reshape(n_dp, n_ctx, cols)
    table_row = jnp.pad(table_part.reshape(-1), (0, cols - table_part.size))
    table_rows = jnp.broadcast_to(table_row[None, None, :], (n_dp, 1, cols))
    extra = jnp.pad(jnp.concatenate([small_grads, table_rows], axis=1), ((0, 0), (0, 16 - n_ctx - 1), (0, 0))).astype(bf16)
    blocks = jnp.concatenate([grad_proj.reshape(n_dp, quarter, cols), extra], axis=1)
    blocks = xor_order([blocks[k] for k in range(n_dp)], d)
    summed = pair_sum([b.astype(f32) for b in [blocks[0]] + [send(blocks[m], "dp", m) for m in dp_peers]]).astype(bf16)
    table_sum = summed[quarter + n_ctx : quarter + n_ctx + 1]
    blocks = [
        jnp.concatenate([summed[k * shard : (k + 1) * shard], summed[quarter + k : quarter + k + 1], table_sum, jnp.zeros((14, cols), bf16)])
        for k in range(n_ctx)
    ]
    blocks = xor_order(blocks, c)
    got = [blocks[0]] + [send(blocks[m], "ctx", m) for m in ctx_peers]
    small_sum = pair_sum([b[shard].astype(f32) for b in got])
    got = xor_order(got, c)
    grad_projections = jnp.concatenate([b[:shard].astype(f32).reshape(shard, 3, group) for b in got], axis=2)
    bias_sum = jnp.concatenate([b[shard + 1, : table_part.size].astype(f32).reshape(2, -1) for b in got]).T
    return (
        output.astype(bf16),
        grad_inputs,
        small_sum[:shard],
        grad_projections,
        grad_output_weight,
        bias_sum,
        small_sum[shard : 2 * shard],
        small_sum[2 * shard :].reshape(shard, experts),
        grad_gate_up,
        grad_down,
    )


def solution(mesh):
    sizes = dict(mesh.shape)
    body = functools.partial(on_device_fast, sizes) if sizes["ctx"] == 4 and sizes["dp"] == 4 else on_device
    return jax.shard_map(
        body,
        mesh=mesh,
        in_specs=(
            P(("dp", "ctx"), None),
            P("dp"),
            P(("dp", "ctx"), None),
            P(("dp", "ctx"), None),
            P(("dp", "ctx")),
            P(("dp", "ctx"), None, "tensor"),
            P(("dp", "ctx"), "tensor"),
            P(None, "tensor"),
            P(("dp", "ctx")),
            P(("dp", "ctx"), None),
            P("dp", "ctx", None, "tensor"),
            P("dp", "ctx", "tensor"),
            P(("dp", "ctx"), None),
        ),
        out_specs=(
            P(("dp", "ctx"), None),
            P(("dp", "ctx"), None),
            P(("dp", "ctx")),
            P(("dp", "ctx"), None, "tensor"),
            P(("dp", "ctx"), "tensor"),
            P(None, "tensor"),
            P(("dp", "ctx")),
            P(("dp", "ctx"), None),
            P("dp", "ctx", None, "tensor"),
            P("dp", "ctx", "tensor"),
        ),
        check_vma=False,
    )
```
